256 devices in a mesh: rows: 32 (over x, z), dim: 8 (over y, core).
Axes of the slice: x: 4, y: 4, z: 8, core: 2. Of those that a mesh axis runs over, the one named last changes fastest.
Arguments:
- embeddings: float32 [256, 512, 128], P('rows', 'dim'), as said below
- prior: float32 [256, 512, 128], P('rows', 'dim'), may hold values from -9 to 9
- neighbours: int32 [256, 16], P('rows'), may hold values from 0 to 255, as said below
- seed_mask: int32 [32768], P('rows'), may hold values 0 or 1
- families: int32 [32768], P('rows'), may hold values from 0 to 511
Outputs:
- log_ratio: float32 [32768, 512], P(('rows', 'dim'))
The draws below stay inside these ranges and needn't reach their ends.
Inputs may be any that keep to these rules, and one draw needn't show every extreme that they name: `neighbours`: each list names 16 different blocks. Together, the lists of the 8 blocks 8g to 8g + 7 of one group name exactly 2 different blocks of every group of 8 blocks. `embeddings`: each row has its own positive scale.
All inputs are finite; a program needn't handle non-finite values. No bound on the sum of `seed_mask` on one device may be relied on, other than what follows from the above.
Results may differ from the reference program's by a relative error of at most 0.00078.
Values may be sent and summed in bfloat16 or wider, within the bound.
No kernel may reach another device: no remote copies, remote signals or barrier semaphores. Data moves between devices by JAX's collectives and lax.ppermute only.
A program may use at most 64 MiB of HBM per device.

```python
import jax
import jax.numpy as jnp
from jax import lax

E = 512
F = 512
BR = 128
NBR = 16
ITERS = 3
GB = 8
NB = 256
N = 32768


def draw_embeddings(key, part):
    first, second, third = jax.random.split(key, 3)
    row_scale = jnp.exp(jax.random.uniform(first, (NB, 1, BR), jnp.float32, 0.0, 2.302585))
    col_scale = jnp.exp(jax.random.uniform(second, (1, E, 1), jnp.float32, 0.0, 2.302585))
    base = jax.random.normal(third, (NB, E, BR), jnp.float32)
    return (base * row_scale * col_scale).astype(jnp.float32)


def draw_neighbours(key, part):
    groups = NB // GB
    slots = GB // 4
    count = groups * slots
    cover = -(-count // NBR)

    def one_group(group_key):
        pick_key, order_key, heat_key, noise_key = jax.random.split(group_key, 4)
        chosen = jax.vmap(lambda inner: jax.random.permutation(inner, GB)[:slots])(jax.random.split(pick_key, groups))
        candidates = (jnp.arange(groups, dtype=jnp.int32)[:, None] * GB + chosen.astype(jnp.int32)).reshape(count)
        sigma = jax.random.permutation(order_key, count).astype(jnp.int32)
        places = jnp.arange(GB, dtype=jnp.int32)[:, None] * NBR + jnp.arange(NBR, dtype=jnp.int32)[None, :]
        cover_list = sigma[places % count]
        heat = jax.random.randint(heat_key, (count,), 0, 8)
        heat = heat * heat
        noise = jax.random.randint(noise_key, (GB, count), 0, 1024)
        score = (heat[None, :] * 1024 + noise) * count + jnp.arange(count, dtype=jnp.int32)[None, :]
        hot_list = lax.top_k(score, NBR)[1].astype(jnp.int32)
        picks = jnp.where(jnp.arange(GB, dtype=jnp.int32)[:, None] < cover, cover_list, hot_list)
        return candidates[picks]
    lists = jax.vmap(one_group)(jax.random.split(key, groups))
    return lists.reshape(NB, NBR).astype(jnp.int32)


def place_ends(values, own_key, least, largest):
    shape = values.shape
    place = [jax.random.randint(jax.random.fold_in(own_key, axis), (), 0, shape[axis]) for axis in range(len(shape))]
    values = values.at[tuple(place)].set(least)
    longest = shape.index(max(shape))
    place[longest] = (place[longest] + 1) % shape[longest]
    return values.at[tuple(place)].set(largest)


def block_levels(key, extent, pieces, least, high):
    loudness, own = 1.0, jax.random.fold_in(key, 6)
    for axis_at, shards_of in pieces:
        steps = jnp.exp(jax.random.uniform(jax.random.fold_in(own, axis_at), (shards_of,), jnp.float32, least / len(pieces), high / len(pieces)))
        loudness = loudness * jnp.repeat(steps, extent[axis_at] // shards_of).reshape([-1 if axis == axis_at else 1 for axis in range(len(extent))])
    return loudness


def normal_values(key, extent, scale, bound, cuts=(), kind=jnp.bfloat16):
    values = jax.random.normal(key, extent, jnp.float32) * scale
    if len(cuts) > 0:
        values = block_levels(key, extent, cuts, -0.22, 0.18) * values
    return jnp.clip(values, min=-bound, max=bound).astype(kind)


def setup_inputs(seed: int = 0) -> dict:
    key_of = jax.random.split(jax.random.key(seed), 6)
    embeddings = draw_embeddings(jax.random.fold_in(key_of[5], 71), 0)
    prior = normal_values(key_of[1], (NB, F, BR), 3.0, 9.0, ((0, 32), (1, 8)), jnp.float32)
    neighbours = draw_neighbours(jax.random.fold_in(key_of[5], 71), 0)
    seed_mask = place_ends((jax.random.randint(key_of[3], (N,), 0, 4) < 1).astype(jnp.int32), jax.random.fold_in(key_of[3], 1), 0, 1)
    families = place_ends(jax.random.randint(key_of[4], (N,), 0, F), jax.random.fold_in(key_of[4], 1), 0, F - 1).astype(jnp.int32)
    return {"embeddings": embeddings, "prior": prior, "neighbours": neighbours, "seed_mask": seed_mask, "families": families}


sharpness = 16.0
seed_weight = 0.5
label_floor = 0.001
norm_eps = 1e-06

def reference(embeddings, prior, neighbours, seed_mask, families):
    rows_major = jnp.transpose(embeddings, (0, 2, 1)).reshape(N, E)
    prior_rows = jnp.transpose(prior, (0, 2, 1)).reshape(N, F)
    squares = lax.optimization_barrier(jnp.sum(rows_major * rows_major, axis=1))
    unit = rows_major * lax.rsqrt(squares + norm_eps)[:, None]
    unit_blocks = unit.reshape(NB, BR, E)

    def block_weights(packed):
        query, listed = packed
        keys = unit_blocks[listed].reshape(NBR * BR, E)
        cosine = jnp.dot(query, keys.T, precision=lax.Precision.HIGHEST, preferred_element_type=jnp.float32)
        raised = jnp.exp(sharpness * (cosine - 1.0))
        return (raised / lax.optimization_barrier(jnp.sum(raised, axis=1, keepdims=True))).astype(jnp.bfloat16)
    weights = lax.map(block_weights, (unit_blocks, neighbours))
    raised_prior = jnp.exp(prior_rows)
    labels = (raised_prior / lax.optimization_barrier(jnp.sum(raised_prior, axis=1, keepdims=True))).astype(jnp.bfloat16)
    labels = labels.reshape(NB, BR, F)
    onehot = (families[:, None] == jnp.arange(F, dtype=jnp.int32)[None, :]).astype(jnp.float32)
    seeds = (seed_weight * seed_mask.astype(jnp.float32)[:, None] * onehot).reshape(NB, BR, F)
    shifted = seeds
    total = seeds
    for sweep in range(ITERS):
        current = labels

        def block_mix(packed):
            weight_block, listed = packed
            near_rows = current[listed].reshape(NBR * BR, F)
            return jnp.dot(weight_block, near_rows, preferred_element_type=jnp.float32)
        mixed = lax.map(block_mix, (weights, neighbours)) + seeds
        shifted = mixed + label_floor
        squared = shifted * shifted
        total = lax.optimization_barrier(jnp.sum(squared, axis=2, keepdims=True))
        if sweep + 1 < ITERS:
            labels = (squared / total).astype(jnp.bfloat16)
    result = 2.0 * jnp.log(shifted) - jnp.log(total) + jnp.log(jnp.float32(F))
    return result.reshape(N, F)
```

```python
import jax
import jax.numpy as jnp
from jax import lax
from jax.experimental import pallas as pl
from jax.experimental.pallas import tpu as pltpu
from jax.sharding import PartitionSpec as P

ITERS = 3
CORES = 2

sharpness = 16.0
seed_weight = 0.5
label_floor = 0.001
norm_eps = 1e-06

F32 = jnp.float32
BF16 = jnp.bfloat16
SMEM = pl.BlockSpec(memory_space=pltpu.SMEM)
VMEM = pl.BlockSpec(memory_space=pltpu.VMEM)


def call(body, outs, specs, *args, scratch=()):
    return pl.pallas_call(
        body,
        out_shape=outs,
        in_specs=specs,
        out_specs=jax.tree.map(lambda _: VMEM, outs),
        scratch_shapes=scratch,
    )(*args)


def raise_prior(prior):
    blocks, fams, rows = prior.shape
    parts = 4

    def body(prior_ref, out_ref):
        for pair in range(blocks // 2):
            both = jnp.exp(prior_ref[2 * pair : 2 * pair + 2]).reshape(2 * fams, rows)
            out_ref[:, pair] = both.T.reshape(parts, rows // parts, 2 * fams)

    return call(
        body,
        jax.ShapeDtypeStruct((parts, blocks // 2, rows // parts, 2 * fams), F32),
        [VMEM],
        prior,
    )


def lanes_of(column):
    return jnp.broadcast_to(column, (column.shape[0], 128)).T[:8]


def column_of(lanes):
    return jnp.broadcast_to(lanes[:1], (128, lanes.shape[1])).T


def gather_prior(came):
    sources, pairs, rows, both = came.shape
    fams = both // 2

    def body(came_ref, out_ref, total_ref):
        for pair in range(pairs):
            for half in range(2):
                wide = jnp.concatenate(
                    [came_ref[s, pair][:, half * fams : half * fams + fams] for s in range(sources)],
                    axis=1,
                )
                out_ref[2 * pair + half] = wide
        whole = out_ref[...].reshape(2 * pairs * rows, sources * fams)
        total_ref[...] = lanes_of(jnp.sum(whole, axis=1, keepdims=True))

    return call(
        body,
        (
            jax.ShapeDtypeStruct((2 * pairs, rows, sources * fams), F32),
            jax.ShapeDtypeStruct((8, 2 * pairs * rows), F32),
        ),
        [VMEM],
        came,
    )


def pick_embeddings(everyone, wanted, first):
    sources, blocks, feats, rows = everyone.shape
    count = wanted.shape[0]
    part = rows // 4

    def body(every_ref, wanted_ref, first_ref, rows_ref, out_ref):
        for block in range(blocks):
            wide = every_ref[:, block].astype(F32).reshape(sources * feats, rows)
            rows_ref[block] = wide.T.astype(BF16)
        start = pl.multiple_of(first_ref[0], part)

        def one(slot, carry):
            out_ref[slot] = rows_ref[wanted_ref[slot], pl.ds(start, part), :]
            return carry

        lax.fori_loop(0, count, one, 0, unroll=8)

    return call(
        body,
        (
            jax.ShapeDtypeStruct((blocks, rows, sources * feats), BF16),
            jax.ShapeDtypeStruct((count, part, sources * feats), BF16),
        ),
        [VMEM, SMEM, SMEM],
        everyone,
        wanted,
        first,
    )


def pick_labels(squared, total, other, wanted):
    blocks, part, fams = squared.shape
    count = wanted.shape[0]

    def body(squared_ref, total_ref, other_ref, wanted_ref, out_ref, labels_ref):
        whole = column_of(total_ref[...] + other_ref[...])
        for block in range(blocks):
            down = whole[block * part : block * part + part]
            down = jnp.concatenate([down] * (fams // 128), axis=1)
            labels_ref[block] = (squared_ref[block] / down).astype(BF16)

        def one(slot, carry):
            out_ref[slot] = labels_ref[wanted_ref[slot]]
            return carry

        lax.fori_loop(0, count, one, 0, unroll=8)

    return call(
        body,
        jax.ShapeDtypeStruct((count, part, fams), BF16),
        [VMEM, VMEM, VMEM, SMEM],
        squared,
        total,
        other,
        wanted,
        scratch=[pltpu.VMEM((blocks, part, fams), BF16)],
    )


def raise_cosines(queries, queries_other, keys, keys_other, flat):
    blocks, rows, feats = queries.shape
    slots, part, _ = keys.shape
    links = flat.shape[0] // blocks

    def body(q_ref, qo_ref, k_ref, ko_ref, flat_ref, out_ref, sum_ref, a_ref, b_ref, n_ref, inv_ref):
        def norm(first, second):
            first, second = first.astype(F32), second.astype(F32)
            squares = jnp.sum(first * first + second * second, axis=1, keepdims=True)
            return lax.rsqrt(squares + norm_eps)

        step = 8
        for at in range(0, slots, step):
            inverse = norm(
                k_ref[at : at + step].reshape(step * part, feats),
                ko_ref[at : at + step].reshape(step * part, feats),
            )
            inv_ref[at : at + step] = jnp.broadcast_to(inverse, (step * part, rows)).reshape(
                step, part, rows
            )
        for block in range(blocks):
            for link in range(links):
                slot = flat_ref[block * links + link]
                a_ref[link * part : link * part + part] = k_ref[slot]
                b_ref[link * part : link * part + part] = ko_ref[slot]
                n_ref[link * part : link * part + part] = inv_ref[slot]
            first, second = q_ref[block], qo_ref[block]
            inverse = jnp.broadcast_to(norm(first, second), (rows, rows)).T[:1]
            dims = (((1,), (1,)), ((), ()))
            product = lax.dot_general(a_ref[...], first, dims, preferred_element_type=F32)
            product += lax.dot_general(b_ref[...], second, dims, preferred_element_type=F32)
            raised = jnp.exp(sharpness * (product * n_ref[...] * inverse - 1.0))
            out_ref[block] = raised
            sum_ref[block : block + 1] = jnp.sum(raised, axis=0, keepdims=True)

    return call(
        body,
        (
            jax.ShapeDtypeStruct((blocks, links * part, rows), F32),
            jax.ShapeDtypeStruct((blocks, rows), F32),
        ),
        [VMEM, VMEM, VMEM, VMEM, SMEM],
        queries,
        queries_other,
        keys,
        keys_other,
        flat,
        scratch=[
            pltpu.VMEM((links * part, feats), BF16),
            pltpu.VMEM((links * part, feats), BF16),
            pltpu.VMEM((links * part, rows), F32),
            pltpu.VMEM((slots, part, rows), F32),
        ],
    )


def weigh(raised, sums):
    blocks, keys, rows = raised.shape

    def body(raised_ref, sums_ref, out_ref):
        total = jnp.sum(sums_ref[...], axis=0)
        for block in range(blocks):
            out_ref[block] = (raised_ref[block] / total[block : block + 1]).T.astype(BF16)

    return call(
        body, jax.ShapeDtypeStruct((blocks, rows, keys), BF16), [VMEM, VMEM], raised, sums
    )


def mix(weights, near, flat, by_slice):
    blocks, rows, keys = weights.shape
    _, part, fams = near.shape
    links = flat.shape[0] // blocks
    slices = rows // part

    def body(weights_ref, near_ref, flat_ref, out_ref, l_ref):
        for block in range(blocks):
            for link in range(links):
                slot = flat_ref[block * links + link]
                l_ref[link * part : link * part + part] = near_ref[slot]
            mixed = jnp.dot(weights_ref[block], l_ref[...], preferred_element_type=F32)
            mixed = mixed.astype(BF16)
            if by_slice:
                out_ref[:, block] = mixed.reshape(slices, part, fams)
            else:
                out_ref[block] = mixed

    shape = (slices, blocks, part, fams) if by_slice else (blocks, rows, fams)
    return call(
        body,
        jax.ShapeDtypeStruct(shape, BF16),
        [VMEM, VMEM, SMEM],
        weights,
        near,
        flat,
        scratch=[pltpu.VMEM((keys, fams), BF16)],
    )


def square(parts, seeds):
    sources, blocks, part, fams = parts.shape

    def body(parts_ref, seeds_ref, out_ref, total_ref):
        mixed = parts_ref[0].astype(F32)
        for source in range(1, sources):
            mixed += parts_ref[source].astype(F32)
        shifted = mixed + seeds_ref[...] + label_floor
        squared = shifted * shifted
        out_ref[...] = squared
        whole = squared.reshape(blocks * part, fams)
        total_ref[...] = lanes_of(jnp.sum(whole, axis=1, keepdims=True))

    return call(
        body,
        (
            jax.ShapeDtypeStruct((blocks, part, fams), F32),
            jax.ShapeDtypeStruct((8, blocks * part), F32),
        ),
        [VMEM, VMEM],
        parts,
        seeds,
    )


def finish(parts, seeds, slab):
    members, rows, fams = parts.shape

    def body(parts_ref, seeds_ref, out_ref):
        halves = []
        for core in range(CORES):
            mixed = parts_ref[core].astype(F32)
            for source in range(core + CORES, members, CORES):
                mixed += parts_ref[source].astype(F32)
            halves.append(mixed + seeds_ref[core] + label_floor)
        total = sum(jnp.sum(half * half, axis=1, keepdims=True) for half in halves)
        last = jnp.log(F32(CORES * fams)) - jnp.log(total)
        for at in range(fams // slab):
            wide = jnp.concatenate(
                [half[:, at * slab : at * slab + slab] for half in halves], axis=1
            )
            out_ref[:, at * CORES * slab : (at + 1) * CORES * slab] = 2.0 * jnp.log(wide) + last

    return call(
        body, jax.ShapeDtypeStruct((rows, CORES * fams), F32), [VMEM, VMEM], parts, seeds
    )


def shards(embeddings, prior, neighbours, seed_mask, families):
    groups = lax.axis_size("rows")
    members = lax.axis_size("dim")
    member = lax.axis_index("dim")
    blocks, links = neighbours.shape
    slab = embeddings.shape[1]
    rows = embeddings.shape[2]
    sides = members // CORES
    side, core = member // CORES, member % CORES
    part = rows // sides
    lines = [[s * CORES + k for s in range(sides)] for k in range(CORES)]
    swap = [(m, m ^ 1) for m in range(members)]

    def over_y(x):
        return lax.all_to_all(
            x, "dim", split_axis=0, concat_axis=0, tiled=True, axis_index_groups=lines
        )

    def over_rows(x):
        return lax.all_to_all(x, "rows", split_axis=0, concat_axis=0, tiled=True)

    def other_core(x):
        return lax.ppermute(x, "dim", swap)

    def across(out):
        return over_rows(out.reshape(groups, out.shape[0] // groups, *out.shape[1:])).reshape(
            out.shape
        )

    lists = neighbours.reshape(blocks * links)
    owner, within = lists // blocks, lists % blocks
    held = owner[None, :] == jnp.arange(groups, dtype=jnp.int32)[:, None]
    low = jnp.min(jnp.where(held, within[None, :], blocks), axis=1)
    high = jnp.max(jnp.where(held, within[None, :], -1), axis=1)
    wanted = over_rows(jnp.stack([low, high], axis=1)).reshape(groups * 2)
    highs = jnp.sum(jnp.where(held, high[:, None], 0), axis=0)
    flat = owner * 2 + (within == highs).astype(jnp.int32)

    rounded = embeddings.astype(BF16)
    everyone = over_y(jnp.broadcast_to(rounded[None], (sides, *rounded.shape)))
    first = (side * part).reshape(1)
    queries, outgoing = pick_embeddings(everyone, wanted, first)
    keys = across(outgoing)
    queries_other = other_core(queries)

    raised_prior, total = gather_prior(over_y(raise_prior(prior)))
    near = across(pick_labels(raised_prior, total, other_core(total), wanted))

    keys_other = other_core(keys)
    raised, sums = raise_cosines(queries, queries_other, keys, keys_other, flat)
    weights = weigh(raised, over_y(jnp.broadcast_to(sums[None], (sides, *sums.shape))))

    at = jnp.arange(sides * slab, dtype=jnp.int32)
    ids = (at // slab) * (CORES * slab) + at % slab

    def seeded(mask, fams, core):
        return (
            seed_weight
            * mask.astype(F32)[..., None]
            * (fams[..., None] == ids + core * slab).astype(F32)
        )

    mask = seed_mask.reshape(blocks, rows)
    fams = families.reshape(blocks, rows)
    seeds = seeded(
        lax.dynamic_slice_in_dim(mask, side * part, part, 1),
        lax.dynamic_slice_in_dim(fams, side * part, part, 1),
        core,
    )
    my_mask = lax.dynamic_index_in_dim(mask, member, 0, keepdims=False)
    my_fams = lax.dynamic_index_in_dim(fams, member, 0, keepdims=False)
    my_seeds = jnp.stack([seeded(my_mask, my_fams, k) for k in range(CORES)])

    for sweep in range(ITERS - 1):
        squared, total = square(over_y(mix(weights, near, flat, True)), seeds)
        near = across(pick_labels(squared, total, other_core(total), wanted))
    parts = lax.all_to_all(
        mix(weights, near, flat, False), "dim", split_axis=0, concat_axis=0, tiled=True
    )
    return finish(parts, my_seeds, slab)


def solution(mesh):
    return jax.shard_map(
        shards,
        mesh=mesh,
        in_specs=(
            P("rows", "dim", None),
            P("rows", "dim", None),
            P("rows", None),
            P("rows"),
            P("rows"),
        ),
        out_specs=P(("rows", "dim"), None),
        check_vma=False,
    )
```
